32 devices in a mesh: shot: 16 (over z, x, core), freq: 2 (over y).
Axes of the slice: x: 2, y: 2, z: 4, core: 2. Of those that a mesh axis runs over, the one named last changes fastest.
Arguments:
- wavefield: bfloat16 [4, 6144, 1024], P('freq', 'shot'), parts along dimension 0, may hold values from -0.8984375 to 0.8984375
- recorded: bfloat16 [6, 2, 2, 6144, 384], P('freq', None, None, 'shot'), parts along dimension 0, may hold values from -6 to 6
- match_filter: bfloat16 [2, 63], replicated, may hold values from -0.5 to 0.5
Outputs:
- demultiple: bfloat16 [6, 2, 2, 6144, 384], P('freq', None, None, 'shot'), parts along dimension 0
The draws below stay inside these ranges and needn't reach their ends.
There are 2 independent parts, one for each index of `freq`. The reference program is written for one: setup_inputs(seed, part) draws one part's arguments, and reference() takes and returns one part's arrays. A program takes and returns all parts, laid end to end along the dimension named above; an argument that names none is the same for every part. Nothing has to cross between parts.
All inputs are finite; a program needn't handle non-finite values.
Results may differ from the reference program's by a relative error of at most 0.0048.
Values may be sent and summed in bfloat16 or wider, within the bound.
A program may use at most 64 MiB of HBM per device.

```python
import jax
import jax.numpy as jnp
from jax import lax

SHOT_DEV = 384
APERTURE = 1024
TAPS = 63
OFFSETS = 3
BLOCKS = 16
SHOTS = 6144


def block_scale(own_key, extent, pieces, smallest, high):
    def one(dim, blocks):
        steps = jax.random.uniform(jax.random.fold_in(jax.random.fold_in(own_key, 6), dim), (blocks,), jnp.float32, smallest / len(pieces), high / len(pieces))
        return jnp.repeat(jnp.exp(steps), extent[dim] // blocks).reshape((-1,) + (1,) * (len(extent) - dim - 1))

    gain = one(*pieces[0])
    for cut in pieces[1:]:
        gain = gain * one(*cut)
    return gain


def scatter_about(rng, shape, width, bound, pieces=(), kind=jnp.bfloat16):
    result = width * jax.random.normal(rng, shape, jnp.float32)
    if pieces:
        result = result * block_scale(rng, shape, pieces, -0.22, 0.18)
    return jnp.clip(result, -bound, bound).astype(kind)


def setup_inputs(seed: int = 0, part: int = 0) -> dict:
    streams_of = jax.random.split(jax.random.key(seed), 4)
    part_splits = jax.random.split(jax.random.fold_in(streams_of[3], part), 4)
    return {
        "wavefield": scatter_about(part_splits[0], (2, SHOTS, APERTURE), 0.15, 0.8984375, ((1, 16),)),
        "recorded": scatter_about(part_splits[1], (OFFSETS, 2, 2, SHOTS, SHOT_DEV), 1.0, 6.0, ((3, 16),)),
        "match_filter": scatter_about(streams_of[2], (2, TAPS), (2 * TAPS) ** -0.5, 0.5),
    }


def toeplitz(match_filter, block_span_width):
    tap_count = match_filter.shape[1]
    half_taps = (tap_count - 1) // 2
    row_index = lax.broadcasted_iota(jnp.int32, (block_span_width, block_span_width), 0)
    col_index = lax.broadcasted_iota(jnp.int32, (block_span_width, block_span_width), 1)
    lag_index = row_index - col_index + half_taps
    coeffs = match_filter.astype(jnp.float32)

    def place_tap(tap_index, carried):
        column = lax.dynamic_slice_in_dim(coeffs, tap_index, 1, 1)
        return jnp.where((lag_index == tap_index)[None], column[:, :, None], carried)

    return lax.fori_loop(0, tap_count, place_tap, jnp.zeros((2, block_span_width, block_span_width), jnp.float32))


def filter_weights(match_filter, block_span_width):
    toe_pair = toeplitz(match_filter, block_span_width)
    real_component = toe_pair[0].astype(jnp.bfloat16)
    imag_part = toe_pair[1].astype(jnp.bfloat16)
    return jnp.stack([jnp.stack([real_component, imag_part], 1), jnp.stack([-imag_part, real_component], 1)], 0)


def reference(wavefield, recorded, match_filter):
    weights = filter_weights(match_filter, SHOT_DEV).astype(jnp.float32)
    every_block = wavefield.astype(jnp.float32).reshape(2, BLOCKS, SHOT_DEV, APERTURE)
    outputs = []
    for slot_index, offset in enumerate((1, BLOCKS // 8, BLOCKS // 4)):
        paired_shot = jnp.roll(every_block, -offset, axis=1)
        real_block_tile = jnp.einsum("ldz,lez->lde", every_block[0], paired_shot[0]) - jnp.einsum("ldz,lez->lde", every_block[1], paired_shot[1])
        imaginary_tile = jnp.einsum("ldz,lez->lde", every_block[0], paired_shot[1]) + jnp.einsum("ldz,lez->lde", every_block[1], paired_shot[0])
        ahead_tiles = jnp.stack([real_block_tile, imaginary_tile], 1).astype(jnp.bfloat16)
        behind_tiles = jnp.swapaxes(jnp.roll(ahead_tiles, offset, axis=0), 2, 3)
        side_list = []
        for side_index, tile_set in enumerate((ahead_tiles, behind_tiles)):
            matched_output = jnp.einsum("bcsq,cqdx->dbsx", tile_set.astype(jnp.float32), weights)
            matched_output = matched_output.reshape(2, SHOTS, SHOT_DEV)
            side_list.append((recorded[slot_index, side_index].astype(jnp.float32) - matched_output).astype(jnp.bfloat16))
        outputs.append(jnp.stack(side_list))
    return jnp.stack(outputs)
```

```python
import functools

import jax
import jax.numpy as jnp
from jax import lax
from jax.experimental import pallas as pl
from jax.experimental.pallas import tpu as pltpu
from jax.sharding import PartitionSpec as P

MESH = pl.DeviceIdType.MESH
STEP = 128
CH_A, CH_B, CH_C, CH_M, CH_D = range(5)
F32 = jnp.float32
BF16 = jnp.bfloat16


def dot_t(a, b):
    return lax.dot_general(a, b, (((1,), (1,)), ((), ())), preferred_element_type=F32)


def kernel(
    n, mf, wave, rec, out,
    left, weights, buf_a, buf_b, buf_c, buf_m, buf_d,
    send_a, send_c, recv_a, recv_c, tile, tile2, tile3, rec_v, res,
    ssem, rsem, in_sem, out_sem,
):
    span, depth = wave.shape[1], wave.shape[2]
    pieces = span // STEP
    taps = mf.shape[1]
    half = (taps - 1) // 2
    me = lax.axis_index("shot")
    core = lax.rem(me, 2)
    side = lax.rem(me // 2, 2)
    mate = me + 1 - 2 * core
    across = me + 2 - 4 * side
    up, down = lax.rem(me + 4, n), lax.rem(me + n - 4, n)
    z_to = (1 - side) * down + side * up
    z_from = (1 - side) * up + side * down
    owner = (core == side)
    giver = (core != side)

    barrier = pltpu.get_barrier_semaphore()
    for other in (mate, across, up, down):
        pl.semaphore_signal(barrier, inc=1, device_id={"shot": other}, device_id_type=MESH)
    pl.semaphore_wait(barrier, 4)

    def remote(src, dst, sem, target):
        return pltpu.make_async_remote_copy(
            src_ref=src, dst_ref=dst, send_sem=ssem.at[sem], recv_sem=rsem.at[sem],
            device_id={"shot": target}, device_id_type=MESH,
        )

    def rows(i):
        if isinstance(i, int):
            return pl.ds(i * STEP, STEP)
        return pl.ds(pl.multiple_of(i * STEP, STEP), STEP)

    def cols(i, base):
        return pl.ds(pl.multiple_of(base + i * STEP, STEP), STEP)

    def piece(src, dst, channel, i, target):
        return remote(
            src.at[:, rows(i), :], dst.at[:, rows(i), :], channel * pieces + i, target
        )

    tile_sem = 5 * pieces

    def z_copy(i):
        return piece(wave, buf_a, CH_A, i, z_to)

    def fwd_copy(i):
        return piece(buf_a, buf_b, CH_B, i, across)

    def row_copy(i):
        return piece(wave, buf_c, CH_C, i, across)

    def mate_copy(i):
        return piece(wave, buf_m, CH_M, i, mate)

    def share_c(i):
        return piece(buf_c, buf_d, CH_D, i, mate)

    def share_b(i):
        return piece(buf_b, buf_d, CH_D, i, mate)

    tile_a = remote(send_a, recv_a, tile_sem, z_from)
    tile_c = remote(send_c, recv_c, tile_sem + 1, across)

    @pl.when(giver)
    def _():
        for i in range(pieces):
            row_copy(i).start()

    for i in range(pieces):
        z_copy(i).start()
    for i in range(pieces):
        mate_copy(i).start()
    load = pltpu.make_async_copy(rec, rec_v, in_sem)
    load.start()

    left[:span, :depth] = wave[0]
    left[:span, depth:] = -wave[1]
    left[span:, :depth] = wave[1]
    left[span:, depth:] = wave[0]

    weights[...] = jnp.zeros_like(weights)
    shape = (STEP, STEP)
    base_lag = lax.broadcasted_iota(jnp.int32, shape, 0) - lax.broadcasted_iota(jnp.int32, shape, 1)
    reach = -(-half // STEP) if half else 0
    for d in range(-reach, reach + 1):
        if abs(d) >= pieces:
            continue
        lag = base_lag + (d * STEP + half)

        def place(tap, carry, lag=lag):
            hit = lag == tap
            return (
                jnp.where(hit, mf[0, tap], carry[0]),
                jnp.where(hit, mf[1, tap], carry[1]),
            )

        zero = jnp.zeros(shape, F32)
        real, imag = lax.fori_loop(0, taps, place, (zero, zero))
        real, imag = real.astype(BF16), imag.astype(BF16)
        for bc in range(pieces):
            br = bc + d
            if 0 <= br < pieces:
                r0, c0 = br * STEP, bc * STEP
                weights[r0:r0 + STEP, c0:c0 + STEP] = real
                weights[r0:r0 + STEP, span + c0:span + c0 + STEP] = imag
                weights[span + r0:span + r0 + STEP, c0:c0 + STEP] = -imag
                weights[span + r0:span + r0 + STEP, span + c0:span + c0 + STEP] = real

    def own_tile(src, dst, i):
        t = dot_t(left[:, :depth], src[0, rows(i), :]) + dot_t(left[:, depth:], src[1, rows(i), :])
        t = t.astype(BF16)
        dst[:, cols(i, 0)] = t[:span]
        dst[:, cols(i, span)] = t[span:]

    def their_tile(src, dst, i):
        t = dot_t(src[0, rows(i), :], left[:, :depth]) + dot_t(src[1, rows(i), :], left[:, depth:])
        dst[rows(i), :] = t.astype(BF16)

    def put(t, k, j):
        return pltpu.make_async_copy(res.at[t, k], out.at[t, k], out_sem.at[j])

    def emit(t, k, src, j):
        f = jnp.dot(src[...], weights[...], preferred_element_type=F32)
        res[t, k, 0] = (rec_v[t, k, 0].astype(F32) - f[:, :span]).astype(BF16)
        res[t, k, 1] = (rec_v[t, k, 1].astype(F32) - f[:, span:]).astype(BF16)
        put(t, k, j).start()

    def each(body):
        def step(i, carry):
            body(i)
            return carry
        lax.fori_loop(0, pieces, step, 0)

    load.wait()

    @each
    def _(i):
        mate_copy(i).wait_recv()
        own_tile(buf_m, tile, i)

    emit(0, core, tile, 0)

    @each
    def _(i):
        @pl.when(owner)
        def _():
            row_copy(i).wait_recv()
            share_c(i).start()

        z_copy(i).wait_recv()
        fwd_copy(i).start()

        @pl.when(owner)
        def _():
            their_tile(buf_c, send_c, i)
        their_tile(buf_a, send_a, i)

        @pl.when(owner)
        def _():
            own_tile(buf_c, tile3, i)
        own_tile(buf_a, tile, i)

    tile_a.start()

    @pl.when(owner)
    def _():
        tile_c.start()
        emit(1, side, tile3, 3)
    emit(2, side, tile, 1)

    @pl.when(giver)
    def _():
        @each
        def _(i):
            share_c(i).wait_recv()
            own_tile(buf_d, tile3, i)
        emit(0, 1 - core, tile3, 4)

    @each
    def _(i):
        fwd_copy(i).wait_recv()

        @pl.when(giver)
        def _():
            share_b(i).start()
        own_tile(buf_b, tile2, i)

        @pl.when(owner)
        def _():
            share_b(i).wait_recv()
            own_tile(buf_d, tile3, i)

    emit(1, 1 - side, tile2, 2)

    @pl.when(owner)
    def _():
        emit(0, 1 - core, tile3, 4)

    tile_a.wait_recv()
    emit(2, 1 - side, recv_a, 5)

    @pl.when(giver)
    def _():
        tile_c.wait_recv()
        emit(1, side, recv_c, 3)

    for i in range(pieces):
        z_copy(i).wait_send()
        fwd_copy(i).wait_send()
        mate_copy(i).wait_send()
        share_c(i).wait_send()
    tile_a.wait_send()

    @pl.when(giver)
    def _():
        for i in range(pieces):
            row_copy(i).wait_send()

    @pl.when(owner)
    def _():
        tile_c.wait_send()

    put(0, core, 0).wait()
    put(2, side, 1).wait()
    put(1, 1 - side, 2).wait()
    put(1, side, 3).wait()
    put(0, 1 - core, 4).wait()
    put(2, 1 - side, 5).wait()


def ladder(wavefield, recorded, match_filter):
    n = lax.axis_size("shot")
    _, span, depth = wavefield.shape
    pieces = span // STEP
    slots = recorded.shape[0]
    block = pltpu.VMEM((2, span, depth), BF16)
    flat = pltpu.VMEM((span, 2 * span), BF16)
    return pl.pallas_call(
        functools.partial(kernel, n),
        out_shape=jax.ShapeDtypeStruct(recorded.shape, recorded.dtype),
        in_specs=[
            pl.BlockSpec(memory_space=pltpu.SMEM),
            pl.BlockSpec(memory_space=pltpu.VMEM),
            pl.BlockSpec(memory_space=pl.ANY),
        ],
        out_specs=pl.BlockSpec(memory_space=pl.ANY),
        scratch_shapes=[
            pltpu.VMEM((2 * span, 2 * depth), BF16),
            pltpu.VMEM((2 * span, 2 * span), BF16),
            block, block, block, block, block,
            flat, flat, flat, flat, flat, flat, flat,
            pltpu.VMEM(recorded.shape, BF16),
            pltpu.VMEM(recorded.shape, BF16),
            pltpu.SemaphoreType.DMA((5 * pieces + 2,)),
            pltpu.SemaphoreType.DMA((5 * pieces + 2,)),
            pltpu.SemaphoreType.DMA,
            pltpu.SemaphoreType.DMA((2 * slots,)),
        ],
        compiler_params=pltpu.CompilerParams(
            collective_id=0, has_side_effects=True, vmem_limit_bytes=56 * 2**20
        ),
    )(match_filter.astype(F32), wavefield, recorded)


def passed_along(value, axis, steps):
    count = lax.axis_size(axis)
    pairs = [(source, (source + steps) % count) for source in range(count)]
    return lax.ppermute(value, axis, pairs)


def toeplitz(match_filter, block_span_width):
    tap_count = match_filter.shape[1]
    half_taps = (tap_count - 1) // 2
    row_index = lax.broadcasted_iota(jnp.int32, (block_span_width, block_span_width), 0)
    col_index = lax.broadcasted_iota(jnp.int32, (block_span_width, block_span_width), 1)
    lag_index = row_index - col_index + half_taps
    coeffs = match_filter.astype(jnp.float32)

    def place_tap(tap_index, carried):
        column = lax.dynamic_slice_in_dim(coeffs, tap_index, 1, 1)
        return jnp.where((lag_index == tap_index)[None], column[:, :, None], carried)

    return lax.fori_loop(
        0, tap_count, place_tap, jnp.zeros((2, block_span_width, block_span_width), jnp.float32)
    )


def filter_weights(match_filter, block_span_width):
    toe_pair = toeplitz(match_filter, block_span_width)
    real_component = toe_pair[0].astype(jnp.bfloat16)
    imag_part = toe_pair[1].astype(jnp.bfloat16)
    return jnp.stack(
        [jnp.stack([real_component, imag_part], 1), jnp.stack([-imag_part, real_component], 1)], 0
    )


def shards(wavefield, recorded, match_filter):
    cycle_size = lax.axis_size("shot")
    doubling = cycle_size // 8 == 2 and cycle_size // 4 == 4
    if doubling and cycle_size % 4 == 0 and wavefield.shape[1] % STEP == 0:
        return ladder(wavefield, recorded, match_filter)
    block_span_width = wavefield.shape[1]
    weights = filter_weights(match_filter, block_span_width)
    real_component = wavefield[0]
    imag_part = wavefield[1]
    left_rows = jnp.concatenate(
        [
            jnp.concatenate([real_component, -imag_part], 1),
            jnp.concatenate([imag_part, real_component], 1),
        ],
        0,
    )
    results = []
    for slot_index, offset in enumerate((1, cycle_size // 8, cycle_size // 4)):
        ahead_data = passed_along(wavefield, "shot", -offset)
        right_rows = jnp.concatenate([ahead_data[0], ahead_data[1]], 1)
        stacked = lax.dot_general(
            left_rows, right_rows, (((1,), (1,)), ((), ())), preferred_element_type=jnp.float32
        )
        forward_tile = stacked.astype(jnp.bfloat16).reshape(2, block_span_width, block_span_width)
        ahead_filtered = jnp.einsum(
            "csq,cqdx->dsx", forward_tile, weights, preferred_element_type=jnp.float32
        )
        received = passed_along(forward_tile, "shot", offset)
        behind_filtered = jnp.einsum(
            "csr,csdx->drx", received, weights, preferred_element_type=jnp.float32
        )
        ahead_out = (recorded[slot_index, 0].astype(jnp.float32) - ahead_filtered).astype(
            jnp.bfloat16
        )
        behind_out = (recorded[slot_index, 1].astype(jnp.float32) - behind_filtered).astype(
            jnp.bfloat16
        )
        results.append(jnp.stack([ahead_out, behind_out]))
    return jnp.stack(results)


def solution(mesh):
    return jax.shard_map(
        shards,
        mesh=mesh,
        in_specs=(P("freq", "shot", None), P("freq", None, None, "shot", None), P()),
        out_specs=P("freq", None, None, "shot", None),
        check_vma=False,
    )
```

```python
import functools

import jax
import jax.numpy as jnp
from jax import lax
from jax.experimental import pallas as pl
from jax.experimental.pallas import tpu as pltpu
from jax.sharding import PartitionSpec as P

MESH = pl.DeviceIdType.MESH
STEP = 128
CH_A, CH_B, CH_C, CH_M, CH_D, CH_TA, CH_TX = range(7)
LIMIT = 40 * 2**20
F32 = jnp.float32
BF16 = jnp.bfloat16


def dot_t(a, b):
    return lax.dot_general(a, b, (((1,), (1,)), ((), ())), preferred_element_type=F32)


def kernel(
    n, mf, wave, rec, out,
    wave_v, left, weights, buf_a, buf_b, buf_c, buf_m, buf_d,
    send_a, send_x, recv_a, recv_x, tile, tile2, tile3, rec_v, res, taps_row,
    ssem, rsem, in_sem, out_sem,
):
    span, depth = wave_v.shape[1], wave_v.shape[2]
    pieces = span // STEP
    half = (mf.shape[1] - 1) // 2
    me = lax.axis_index("shot")
    core = lax.rem(me, 2)
    side = lax.rem(me // 2, 2)
    mate = me + 1 - 2 * core
    across = me + 2 - 4 * side
    beyond = lax.rem(me + n - 2 + 4 * side, n)
    up, down = lax.rem(me + 4, n), lax.rem(me + n - 4, n)
    z_to = (1 - side) * down + side * up
    z_from = (1 - side) * up + side * down
    owner = (core == side)
    giver = (core != side)

    load_wave = pltpu.make_async_copy(wave, wave_v, in_sem.at[0])
    load_wave.start()
    load = pltpu.make_async_copy(rec, rec_v, in_sem.at[1])
    load.start()

    barrier = pltpu.get_barrier_semaphore()
    for other in (mate, across, beyond, up, down):
        pl.semaphore_signal(barrier, inc=1, device_id={"shot": other}, device_id_type=MESH)
    pl.semaphore_wait(barrier, 5)

    def remote(src, dst, sem, target):
        return pltpu.make_async_remote_copy(
            src_ref=src, dst_ref=dst, send_sem=ssem.at[sem], recv_sem=rsem.at[sem],
            device_id={"shot": target}, device_id_type=MESH,
        )

    def rows(i):
        if isinstance(i, int):
            return pl.ds(i * STEP, STEP)
        return pl.ds(pl.multiple_of(i * STEP, STEP), STEP)

    def cols(i, base):
        return pl.ds(pl.multiple_of(base + i * STEP, STEP), STEP)

    def piece(src, dst, channel, i, target):
        return remote(
            src.at[:, rows(i), :], dst.at[:, rows(i), :], channel * pieces + i, target
        )

    def tile_piece(src, dst, channel, i, target):
        return remote(src.at[rows(i), :], dst.at[rows(i), :], channel * pieces + i, target)

    def z_copy(i):
        return piece(wave, buf_a, CH_A, i, z_to)

    def fwd_copy(i):
        return piece(buf_a, buf_b, CH_B, i, across)

    def row_copy(i):
        return piece(wave, buf_c, CH_C, i, across)

    def mate_copy(i):
        return piece(wave, buf_m, CH_M, i, mate)

    def share_c(i):
        return piece(buf_c, buf_d, CH_D, i, mate)

    def share_b(i):
        return piece(buf_b, buf_d, CH_D, i, mate)

    def tile_a(i):
        return tile_piece(send_a, recv_a, CH_TA, i, z_from)

    def tile_b(i):
        return tile_piece(send_x, recv_x, CH_TX, i, beyond)

    def tile_c(i):
        return tile_piece(send_x, recv_x, CH_TX, i, across)

    @pl.when(giver)
    def _():
        for i in range(pieces):
            row_copy(i).start()

    for i in range(pieces):
        z_copy(i).start()
    for i in range(pieces):
        mate_copy(i).start()

    width = taps_row.shape[1]
    taps_row[...] = jnp.zeros_like(taps_row)
    taps_row[0:2, 0:mf.shape[1]] = mf[...].astype(F32)
    row_id = lax.broadcasted_iota(jnp.int32, (span, width), 0)
    banded = []
    for c in range(2):
        x = jnp.broadcast_to(taps_row[c:c + 1, :], (span, width))
        x = pltpu.roll(x, width - half, 1)
        bit = 1
        while bit < span:
            x = jnp.where((row_id // bit) % 2 == 1, pltpu.roll(x, bit, 1), x)
            bit *= 2
        banded.append(x[:, :span].astype(BF16))
    weights[:span, :span] = banded[0]
    weights[:span, span:] = -banded[1]
    weights[span:, :span] = banded[1]
    weights[span:, span:] = banded[0]

    load_wave.wait()
    left[:span, :depth] = wave_v[0]
    left[:span, depth:] = -wave_v[1]
    left[span:, :depth] = wave_v[1]
    left[span:, depth:] = wave_v[0]

    def own_tile(src, dst, i):
        t = dot_t(left[:, :depth], src[0, rows(i), :]) + dot_t(left[:, depth:], src[1, rows(i), :])
        t = t.astype(BF16)
        dst[:, cols(i, 0)] = t[:span]
        dst[:, cols(i, span)] = t[span:]

    def their_tile(src, dst, i):
        t = dot_t(src[0, rows(i), :], left[:, :depth]) + dot_t(src[1, rows(i), :], left[:, depth:])
        dst[rows(i), :] = t.astype(BF16)

    def put(t, k, i, j):
        return pltpu.make_async_copy(
            res.at[t, k, :, rows(i), :], out.at[t, k, :, rows(i), :], out_sem.at[j * pieces + i]
        )

    def emit(t, k, src, i, j):
        f = dot_t(src[rows(i), :], weights[...])
        res[t, k, 0, rows(i), :] = (rec_v[t, k, 0, rows(i), :].astype(F32) - f[:, :span]).astype(BF16)
        res[t, k, 1, rows(i), :] = (rec_v[t, k, 1, rows(i), :].astype(F32) - f[:, span:]).astype(BF16)
        put(t, k, i, j).start()

    def each(body):
        def step(i, carry):
            body(i)
            return carry
        lax.fori_loop(0, pieces, step, 0)

    load.wait()

    @each
    def _(i):
        mate_copy(i).wait_recv()
        own_tile(buf_m, tile, i)

    each(lambda i: emit(0, core, tile, i, 0))

    @pl.when(owner)
    def _():
        @each
        def _(i):
            row_copy(i).wait_recv()
            share_c(i).start()
            z_copy(i).wait_recv()
            fwd_copy(i).start()
            their_tile(buf_c, send_x, i)
            tile_c(i).start()
            their_tile(buf_a, send_a, i)
            tile_a(i).start()
            own_tile(buf_c, tile3, i)
            own_tile(buf_a, tile, i)

        @each
        def _(i):
            emit(1, side, tile3, i, 3)
            emit(2, side, tile, i, 1)

        @each
        def _(i):
            share_b(i).wait_recv()
            own_tile(buf_d, tile2, i)

        each(lambda i: emit(0, 1 - core, tile2, i, 4))

        @each
        def _(i):
            tile_a(i).wait_recv()
            emit(2, 1 - side, recv_a, i, 5)
            tile_b(i).wait_recv()
            emit(1, 1 - side, recv_x, i, 2)

        @each
        def _(i):
            share_c(i).wait_send()
            fwd_copy(i).wait_send()
            tile_c(i).wait_send()

    @pl.when(giver)
    def _():
        @each
        def _(i):
            z_copy(i).wait_recv()
            their_tile(buf_a, send_a, i)
            tile_a(i).start()
            own_tile(buf_a, tile, i)
            share_c(i).wait_recv()
            own_tile(buf_d, tile3, i)
            fwd_copy(i).wait_recv()
            share_b(i).start()
            their_tile(buf_b, send_x, i)
            tile_b(i).start()
            own_tile(buf_b, tile2, i)

        @each
        def _(i):
            emit(2, side, tile, i, 1)
            emit(0, 1 - core, tile3, i, 4)
            emit(1, 1 - side, tile2, i, 2)

        @each
        def _(i):
            tile_c(i).wait_recv()
            emit(1, side, recv_x, i, 3)

        @each
        def _(i):
            tile_a(i).wait_recv()
            emit(2, 1 - side, recv_a, i, 5)

        @each
        def _(i):
            row_copy(i).wait_send()
            share_b(i).wait_send()
            tile_b(i).wait_send()

    @each
    def _(i):
        z_copy(i).wait_send()
        mate_copy(i).wait_send()
        tile_a(i).wait_send()
        put(0, core, i, 0).wait()
        put(2, side, i, 1).wait()
        put(1, 1 - side, i, 2).wait()
        put(1, side, i, 3).wait()
        put(0, 1 - core, i, 4).wait()
        put(2, 1 - side, i, 5).wait()


def ladder(wavefield, recorded, match_filter):
    n = lax.axis_size("shot")
    _, span, depth = wavefield.shape
    pieces = span // STEP
    slots = recorded.shape[0]
    width = -(-(span + match_filter.shape[1]) // STEP) * STEP
    block = pltpu.VMEM((2, span, depth), BF16)
    flat = pltpu.VMEM((span, 2 * span), BF16)
    return pl.pallas_call(
        functools.partial(kernel, n),
        out_shape=jax.ShapeDtypeStruct(recorded.shape, recorded.dtype),
        in_specs=[
            pl.BlockSpec(memory_space=pltpu.VMEM),
            pl.BlockSpec(memory_space=pltpu.HBM),
            pl.BlockSpec(memory_space=pltpu.HBM),
        ],
        out_specs=pl.BlockSpec(memory_space=pl.ANY),
        scratch_shapes=[
            block,
            pltpu.VMEM((2 * span, 2 * depth), BF16),
            pltpu.VMEM((2 * span, 2 * span), BF16),
            block, block, block, block, block,
            flat, flat, flat, flat, flat, flat, flat,
            pltpu.VMEM(recorded.shape, BF16),
            pltpu.VMEM(recorded.shape, BF16),
            pltpu.VMEM((8, width), F32),
            pltpu.SemaphoreType.DMA((7 * pieces,)),
            pltpu.SemaphoreType.DMA((7 * pieces,)),
            pltpu.SemaphoreType.DMA((2,)),
            pltpu.SemaphoreType.DMA((2 * slots * pieces,)),
        ],
        compiler_params=pltpu.CompilerParams(
            collective_id=0, has_side_effects=True, vmem_limit_bytes=LIMIT
        ),
    )(match_filter, wavefield, recorded)


def passed_along(value, axis, steps):
    count = lax.axis_size(axis)
    pairs = [(source, (source + steps) % count) for source in range(count)]
    return lax.ppermute(value, axis, pairs)


def toeplitz(match_filter, block_span_width):
    tap_count = match_filter.shape[1]
    half_taps = (tap_count - 1) // 2
    row_index = lax.broadcasted_iota(jnp.int32, (block_span_width, block_span_width), 0)
    col_index = lax.broadcasted_iota(jnp.int32, (block_span_width, block_span_width), 1)
    lag_index = row_index - col_index + half_taps
    coeffs = match_filter.astype(jnp.float32)

    def place_tap(tap_index, carried):
        column = lax.dynamic_slice_in_dim(coeffs, tap_index, 1, 1)
        return jnp.where((lag_index == tap_index)[None], column[:, :, None], carried)

    return lax.fori_loop(
        0, tap_count, place_tap, jnp.zeros((2, block_span_width, block_span_width), jnp.float32)
    )


def filter_weights(match_filter, block_span_width):
    toe_pair = toeplitz(match_filter, block_span_width)
    real_component = toe_pair[0].astype(jnp.bfloat16)
    imag_part = toe_pair[1].astype(jnp.bfloat16)
    return jnp.stack(
        [jnp.stack([real_component, imag_part], 1), jnp.stack([-imag_part, real_component], 1)], 0
    )


def shards(wavefield, recorded, match_filter):
    cycle_size = lax.axis_size("shot")
    doubling = cycle_size // 8 == 2 and cycle_size // 4 == 4
    if doubling and cycle_size % 4 == 0 and wavefield.shape[1] % STEP == 0:
        return ladder(wavefield, recorded, match_filter)
    block_span_width = wavefield.shape[1]
    weights = filter_weights(match_filter, block_span_width)
    real_component = wavefield[0]
    imag_part = wavefield[1]
    left_rows = jnp.concatenate(
        [
            jnp.concatenate([real_component, -imag_part], 1),
            jnp.concatenate([imag_part, real_component], 1),
        ],
        0,
    )
    results = []
    for slot_index, offset in enumerate((1, cycle_size // 8, cycle_size // 4)):
        ahead_data = passed_along(wavefield, "shot", -offset)
        right_rows = jnp.concatenate([ahead_data[0], ahead_data[1]], 1)
        stacked = lax.dot_general(
            left_rows, right_rows, (((1,), (1,)), ((), ())), preferred_element_type=jnp.float32
        )
        forward_tile = stacked.astype(jnp.bfloat16).reshape(2, block_span_width, block_span_width)
        ahead_filtered = jnp.einsum(
            "csq,cqdx->dsx", forward_tile, weights, preferred_element_type=jnp.float32
        )
        received = passed_along(forward_tile, "shot", offset)
        behind_filtered = jnp.einsum(
            "csr,csdx->drx", received, weights, preferred_element_type=jnp.float32
        )
        ahead_out = (recorded[slot_index, 0].astype(jnp.float32) - ahead_filtered).astype(
            jnp.bfloat16
        )
        behind_out = (recorded[slot_index, 1].astype(jnp.float32) - behind_filtered).astype(
            jnp.bfloat16
        )
        results.append(jnp.stack([ahead_out, behind_out]))
    return jnp.stack(results)


def solution(mesh):
    return jax.shard_map(
        shards,
        mesh=mesh,
        in_specs=(P("freq", "shot", None), P("freq", None, None, "shot", None), P()),
        out_specs=P("freq", None, None, "shot", None),
        check_vma=False,
    )
```

```python
import functools

import jax
import jax.numpy as jnp
from jax import lax
from jax.experimental import pallas as pl
from jax.experimental.pallas import tpu as pltpu
from jax.sharding import PartitionSpec as P

MESH = pl.DeviceIdType.MESH
STEP = 128
CH_A, CH_B, CH_C, CH_M, CH_D, CH_TA, CH_TX = range(7)
LIMIT = 40 * 2**20
F32 = jnp.float32
BF16 = jnp.bfloat16


def dot_t(a, b):
    return lax.dot_general(a, b, (((1,), (1,)), ((), ())), preferred_element_type=F32)


def kernel(
    n, mf_hbm, wave, rec, out,
    mf, wave_v, left, weights, buf_a, buf_b, buf_c, buf_m, buf_d,
    send_a, send_x, recv_a, recv_x, tile, tile2, tile3, rec_v, res, taps_row,
    ssem, rsem, in_sem, out_sem,
):
    span, depth = wave_v.shape[1], wave_v.shape[2]
    pieces = span // STEP
    half = (mf.shape[1] - 1) // 2
    me = lax.axis_index("shot")
    core = lax.rem(me, 2)
    side = lax.rem(me // 2, 2)
    mate = me + 1 - 2 * core
    across = me + 2 - 4 * side
    beyond = lax.rem(me + n - 2 + 4 * side, n)
    up, down = lax.rem(me + 4, n), lax.rem(me + n - 4, n)
    z_to = (1 - side) * down + side * up
    z_from = (1 - side) * up + side * down
    owner = (core == side)
    giver = (core != side)

    load_taps = pltpu.make_async_copy(mf_hbm, mf, in_sem.at[2])
    load_taps.start()
    load_wave = pltpu.make_async_copy(wave, wave_v, in_sem.at[0])
    load_wave.start()
    load = pltpu.make_async_copy(rec, rec_v, in_sem.at[1])
    load.start()

    barrier = pltpu.get_barrier_semaphore()
    for other in (mate, across, beyond, up, down):
        pl.semaphore_signal(barrier, inc=1, device_id={"shot": other}, device_id_type=MESH)
    pl.semaphore_wait(barrier, 5)

    def remote(src, dst, sem, target):
        return pltpu.make_async_remote_copy(
            src_ref=src, dst_ref=dst, send_sem=ssem.at[sem], recv_sem=rsem.at[sem],
            device_id={"shot": target}, device_id_type=MESH,
        )

    def rows(i):
        if isinstance(i, int):
            return pl.ds(i * STEP, STEP)
        return pl.ds(pl.multiple_of(i * STEP, STEP), STEP)

    def cols(i, base):
        return pl.ds(pl.multiple_of(base + i * STEP, STEP), STEP)

    def piece(src, dst, channel, i, target):
        return remote(
            src.at[:, rows(i), :], dst.at[:, rows(i), :], channel * pieces + i, target
        )

    def tile_piece(src, dst, channel, i, target):
        return remote(src.at[rows(i), :], dst.at[rows(i), :], channel * pieces + i, target)

    def z_copy(i):
        return piece(wave, buf_a, CH_A, i, z_to)

    def fwd_copy(i):
        return piece(buf_a, buf_b, CH_B, i, across)

    def row_copy(i):
        return piece(wave, buf_c, CH_C, i, across)

    def mate_copy(i):
        return piece(wave, buf_m, CH_M, i, mate)

    def share_c(i):
        return piece(buf_c, buf_d, CH_D, i, mate)

    def share_b(i):
        return piece(buf_b, buf_d, CH_D, i, mate)

    def tile_a(i):
        return tile_piece(send_a, recv_a, CH_TA, i, z_from)

    def tile_b(i):
        return tile_piece(send_x, recv_x, CH_TX, i, beyond)

    def tile_c(i):
        return tile_piece(send_x, recv_x, CH_TX, i, across)

    @pl.when(giver)
    def _():
        for i in range(pieces):
            row_copy(i).start()

    for i in range(pieces):
        z_copy(i).start()
    for i in range(pieces):
        mate_copy(i).start()

    load_taps.wait()
    width = taps_row.shape[1]
    taps_row[...] = jnp.zeros_like(taps_row)
    taps_row[0:2, 0:mf.shape[1]] = mf[...].astype(F32)
    row_id = lax.broadcasted_iota(jnp.int32, (span, width), 0)
    banded = []
    for c in range(2):
        x = jnp.broadcast_to(taps_row[c:c + 1, :], (span, width))
        x = pltpu.roll(x, width - half, 1)
        bit = 1
        while bit < span:
            x = jnp.where((row_id // bit) % 2 == 1, pltpu.roll(x, bit, 1), x)
            bit *= 2
        banded.append(x[:, :span].astype(BF16))
    weights[:span, :span] = banded[0]
    weights[:span, span:] = -banded[1]
    weights[span:, :span] = banded[1]
    weights[span:, span:] = banded[0]

    load_wave.wait()
    left[:span, :depth] = wave_v[0]
    left[:span, depth:] = -wave_v[1]
    left[span:, :depth] = wave_v[1]
    left[span:, depth:] = wave_v[0]

    def own_tile(src, dst, i):
        t = dot_t(left[:, :depth], src[0, rows(i), :]) + dot_t(left[:, depth:], src[1, rows(i), :])
        t = t.astype(BF16)
        dst[:, cols(i, 0)] = t[:span]
        dst[:, cols(i, span)] = t[span:]

    def their_tile(src, dst, i):
        t = dot_t(src[0, rows(i), :], left[:, :depth]) + dot_t(src[1, rows(i), :], left[:, depth:])
        dst[rows(i), :] = t.astype(BF16)

    def put(t, k, i, j):
        return pltpu.make_async_copy(
            res.at[t, k, :, rows(i), :], out.at[t, k, :, rows(i), :], out_sem.at[j * pieces + i]
        )

    def emit(t, k, src, i, j):
        f = dot_t(src[rows(i), :], weights[...])
        res[t, k, 0, rows(i), :] = (rec_v[t, k, 0, rows(i), :].astype(F32) - f[:, :span]).astype(BF16)
        res[t, k, 1, rows(i), :] = (rec_v[t, k, 1, rows(i), :].astype(F32) - f[:, span:]).astype(BF16)
        put(t, k, i, j).start()

    def each(body):
        def step(i, carry):
            body(i)
            return carry
        lax.fori_loop(0, pieces, step, 0)

    load.wait()

    @each
    def _(i):
        mate_copy(i).wait_recv()
        own_tile(buf_m, tile, i)

    each(lambda i: emit(0, core, tile, i, 0))

    @pl.when(owner)
    def _():
        @each
        def _(i):
            row_copy(i).wait_recv()
            share_c(i).start()
            z_copy(i).wait_recv()
            fwd_copy(i).start()
            their_tile(buf_c, send_x, i)
            tile_c(i).start()
            their_tile(buf_a, send_a, i)
            tile_a(i).start()
            own_tile(buf_c, tile3, i)
            own_tile(buf_a, tile, i)

        @each
        def _(i):
            emit(1, side, tile3, i, 3)
            emit(2, side, tile, i, 1)

        @each
        def _(i):
            share_b(i).wait_recv()
            own_tile(buf_d, tile2, i)

        each(lambda i: emit(0, 1 - core, tile2, i, 4))

        @each
        def _(i):
            tile_a(i).wait_recv()
            emit(2, 1 - side, recv_a, i, 5)
            tile_b(i).wait_recv()
            emit(1, 1 - side, recv_x, i, 2)

        @each
        def _(i):
            share_c(i).wait_send()
            fwd_copy(i).wait_send()
            tile_c(i).wait_send()

    @pl.when(giver)
    def _():
        @each
        def _(i):
            z_copy(i).wait_recv()
            their_tile(buf_a, send_a, i)
            tile_a(i).start()
            own_tile(buf_a, tile, i)
            share_c(i).wait_recv()
            own_tile(buf_d, tile3, i)
            fwd_copy(i).wait_recv()
            share_b(i).start()
            their_tile(buf_b, send_x, i)
            tile_b(i).start()
            own_tile(buf_b, tile2, i)

        @each
        def _(i):
            emit(2, side, tile, i, 1)
            emit(0, 1 - core, tile3, i, 4)
            emit(1, 1 - side, tile2, i, 2)

        @each
        def _(i):
            tile_c(i).wait_recv()
            emit(1, side, recv_x, i, 3)

        @each
        def _(i):
            tile_a(i).wait_recv()
            emit(2, 1 - side, recv_a, i, 5)

        @each
        def _(i):
            row_copy(i).wait_send()
            share_b(i).wait_send()
            tile_b(i).wait_send()

    @each
    def _(i):
        z_copy(i).wait_send()
        mate_copy(i).wait_send()
        tile_a(i).wait_send()
        put(0, core, i, 0).wait()
        put(2, side, i, 1).wait()
        put(1, 1 - side, i, 2).wait()
        put(1, side, i, 3).wait()
        put(0, 1 - core, i, 4).wait()
        put(2, 1 - side, i, 5).wait()


def ladder(wavefield, recorded, match_filter):
    n = lax.axis_size("shot")
    _, span, depth = wavefield.shape
    pieces = span // STEP
    slots = recorded.shape[0]
    width = -(-(span + match_filter.shape[1]) // STEP) * STEP
    block = pltpu.VMEM((2, span, depth), BF16)
    flat = pltpu.VMEM((span, 2 * span), BF16)
    return pl.pallas_call(
        functools.partial(kernel, n),
        out_shape=jax.ShapeDtypeStruct(recorded.shape, recorded.dtype),
        in_specs=[
            pl.BlockSpec(memory_space=pltpu.HBM),
            pl.BlockSpec(memory_space=pltpu.HBM),
            pl.BlockSpec(memory_space=pltpu.HBM),
        ],
        out_specs=pl.BlockSpec(memory_space=pl.ANY),
        scratch_shapes=[
            pltpu.VMEM(match_filter.shape, BF16),
            block,
            pltpu.VMEM((2 * span, 2 * depth), BF16),
            pltpu.VMEM((2 * span, 2 * span), BF16),
            block, block, block, block, block,
            flat, flat, flat, flat, flat, flat, flat,
            pltpu.VMEM(recorded.shape, BF16),
            pltpu.VMEM(recorded.shape, BF16),
            pltpu.VMEM((8, width), F32),
            pltpu.SemaphoreType.DMA((7 * pieces,)),
            pltpu.SemaphoreType.DMA((7 * pieces,)),
            pltpu.SemaphoreType.DMA((3,)),
            pltpu.SemaphoreType.DMA((2 * slots * pieces,)),
        ],
        compiler_params=pltpu.CompilerParams(
            collective_id=0, has_side_effects=True, vmem_limit_bytes=LIMIT
        ),
    )(*(pltpu.with_memory_space_constraint(x, pltpu.HBM) for x in (match_filter, wavefield, recorded)))


def passed_along(value, axis, steps):
    count = lax.axis_size(axis)
    pairs = [(source, (source + steps) % count) for source in range(count)]
    return lax.ppermute(value, axis, pairs)


def toeplitz(match_filter, block_span_width):
    tap_count = match_filter.shape[1]
    half_taps = (tap_count - 1) // 2
    row_index = lax.broadcasted_iota(jnp.int32, (block_span_width, block_span_width), 0)
    col_index = lax.broadcasted_iota(jnp.int32, (block_span_width, block_span_width), 1)
    lag_index = row_index - col_index + half_taps
    coeffs = match_filter.astype(jnp.float32)

    def place_tap(tap_index, carried):
        column = lax.dynamic_slice_in_dim(coeffs, tap_index, 1, 1)
        return jnp.where((lag_index == tap_index)[None], column[:, :, None], carried)

    return lax.fori_loop(
        0, tap_count, place_tap, jnp.zeros((2, block_span_width, block_span_width), jnp.float32)
    )


def filter_weights(match_filter, block_span_width):
    toe_pair = toeplitz(match_filter, block_span_width)
    real_component = toe_pair[0].astype(jnp.bfloat16)
    imag_part = toe_pair[1].astype(jnp.bfloat16)
    return jnp.stack(
        [jnp.stack([real_component, imag_part], 1), jnp.stack([-imag_part, real_component], 1)], 0
    )


def shards(wavefield, recorded, match_filter):
    cycle_size = lax.axis_size("shot")
    doubling = cycle_size // 8 == 2 and cycle_size // 4 == 4
    if doubling and cycle_size % 4 == 0 and wavefield.shape[1] % STEP == 0:
        return ladder(wavefield, recorded, match_filter)
    block_span_width = wavefield.shape[1]
    weights = filter_weights(match_filter, block_span_width)
    real_component = wavefield[0]
    imag_part = wavefield[1]
    left_rows = jnp.concatenate(
        [
            jnp.concatenate([real_component, -imag_part], 1),
            jnp.concatenate([imag_part, real_component], 1),
        ],
        0,
    )
    results = []
    for slot_index, offset in enumerate((1, cycle_size // 8, cycle_size // 4)):
        ahead_data = passed_along(wavefield, "shot", -offset)
        right_rows = jnp.concatenate([ahead_data[0], ahead_data[1]], 1)
        stacked = lax.dot_general(
            left_rows, right_rows, (((1,), (1,)), ((), ())), preferred_element_type=jnp.float32
        )
        forward_tile = stacked.astype(jnp.bfloat16).reshape(2, block_span_width, block_span_width)
        ahead_filtered = jnp.einsum(
            "csq,cqdx->dsx", forward_tile, weights, preferred_element_type=jnp.float32
        )
        received = passed_along(forward_tile, "shot", offset)
        behind_filtered = jnp.einsum(
            "csr,csdx->drx", received, weights, preferred_element_type=jnp.float32
        )
        ahead_out = (recorded[slot_index, 0].astype(jnp.float32) - ahead_filtered).astype(
            jnp.bfloat16
        )
        behind_out = (recorded[slot_index, 1].astype(jnp.float32) - behind_filtered).astype(
            jnp.bfloat16
        )
        results.append(jnp.stack([ahead_out, behind_out]))
    return jnp.stack(results)


def solution(mesh):
    return jax.shard_map(
        shards,
        mesh=mesh,
        in_specs=(P("freq", "shot", None), P("freq", None, None, "shot", None), P()),
        out_specs=P("freq", None, None, "shot", None),
        check_vma=False,
    )
```

```python
import functools

import jax
import jax.numpy as jnp
from jax import lax
from jax.experimental import pallas as pl
from jax.experimental.pallas import tpu as pltpu
from jax.sharding import PartitionSpec as P

MESH = pl.DeviceIdType.MESH
STEP = 128
CH_A, CH_B, CH_C, CH_M, CH_D, CH_TA, CH_TX = range(7)
LIMIT = 40 * 2**20
F32 = jnp.float32
BF16 = jnp.bfloat16


def dot_t(a, b):
    return lax.dot_general(a, b, (((1,), (1,)), ((), ())), preferred_element_type=F32)


def kernel(
    n, mf_hbm, wave, rec, out,
    mf, wave_v, left, weights, buf_a, buf_b, buf_c, buf_m, buf_d,
    send_a, send_x, recv_a, recv_x, tile, tile2, tile3, rec_v, res, taps_row,
    ssem, rsem, in_sem, out_sem, go_sem,
):
    span, depth = wave_v.shape[1], wave_v.shape[2]
    pieces = span // STEP
    half = (mf.shape[1] - 1) // 2
    me = lax.axis_index("shot")
    core = lax.rem(me, 2)
    side = lax.rem(me // 2, 2)
    mate = me + 1 - 2 * core
    across = me + 2 - 4 * side
    beyond = lax.rem(me + n - 2 + 4 * side, n)
    up, down = lax.rem(me + 4, n), lax.rem(me + n - 4, n)
    z_to = (1 - side) * down + side * up
    z_from = (1 - side) * up + side * down
    owner = (core == side)
    giver = (core != side)

    load_taps = pltpu.make_async_copy(mf_hbm, mf, in_sem.at[2])
    load_taps.start()
    load_wave = pltpu.make_async_copy(wave, wave_v, in_sem.at[0])
    load_wave.start()
    load = pltpu.make_async_copy(rec, rec_v, in_sem.at[1])
    load.start()

    barrier = pltpu.get_barrier_semaphore()
    for other in (mate, across, beyond, up, down):
        pl.semaphore_signal(barrier, inc=1, device_id={"shot": other}, device_id_type=MESH)
    pl.semaphore_wait(barrier, 5)

    def remote(src, dst, sem, target):
        return pltpu.make_async_remote_copy(
            src_ref=src, dst_ref=dst, send_sem=ssem.at[sem], recv_sem=rsem.at[sem],
            device_id={"shot": target}, device_id_type=MESH,
        )

    def rows(i):
        if isinstance(i, int):
            return pl.ds(i * STEP, STEP)
        return pl.ds(pl.multiple_of(i * STEP, STEP), STEP)

    def cols(i, base):
        return pl.ds(pl.multiple_of(base + i * STEP, STEP), STEP)

    def piece(src, dst, channel, i, target):
        return remote(
            src.at[:, rows(i), :], dst.at[:, rows(i), :], channel * pieces + i, target
        )

    def tile_piece(src, dst, channel, i, target):
        return remote(src.at[rows(i), :], dst.at[rows(i), :], channel * pieces + i, target)

    def z_copy(i):
        return piece(wave, buf_a, CH_A, i, z_to)

    def fwd_copy(i):
        return piece(buf_a, buf_b, CH_B, i, across)

    def row_copy(i):
        return piece(wave, buf_c, CH_C, i, across)

    def mate_copy(i):
        return piece(wave, buf_m, CH_M, i, mate)

    def share_c(i):
        return piece(buf_c, buf_d, CH_D, i, mate)

    def share_b(i):
        return piece(buf_b, buf_d, CH_D, i, mate)

    def tile_a(i):
        return tile_piece(send_a, recv_a, CH_TA, i, z_from)

    tail = pl.ds(STEP, span - STEP)

    def tile_b(i):
        return remote(
            send_x.at[:, rows(i), tail], recv_x.at[:, rows(i), tail], CH_TX * pieces + i, beyond
        )

    def tile_c(i):
        return piece(send_x, recv_x, CH_TX, i, across)

    @pl.when(giver)
    def _():
        for i in range(pieces):
            row_copy(i).start()

    @pl.when(owner)
    def _():
        for i in range(pieces):
            z_copy(i).start()

    for i in range(pieces):
        mate_copy(i).start()

    load_taps.wait()
    width = taps_row.shape[1]
    taps_row[...] = jnp.zeros_like(taps_row)
    taps_row[0:2, 0:mf.shape[1]] = mf[...].astype(F32)
    row_id = lax.broadcasted_iota(jnp.int32, (span, width), 0)
    banded = []
    for c in range(2):
        x = jnp.broadcast_to(taps_row[c:c + 1, :], (span, width))
        x = pltpu.roll(x, width - half, 1)
        bit = 1
        while bit < span:
            x = jnp.where((row_id // bit) % 2 == 1, pltpu.roll(x, bit, 1), x)
            bit *= 2
        banded.append(x[:, :span].astype(BF16))
    weights[:span, :span] = banded[0]
    weights[:span, span:] = -banded[1]
    weights[span:, :span] = banded[1]
    weights[span:, span:] = banded[0]

    load_wave.wait()
    left[:span, :depth] = wave_v[0]
    left[:span, depth:] = -wave_v[1]
    left[span:, :depth] = wave_v[1]
    left[span:, depth:] = wave_v[0]

    def own_tile(src, dst, i):
        t = dot_t(left[:, :depth], src[0, rows(i), :]) + dot_t(left[:, depth:], src[1, rows(i), :])
        t = t.astype(BF16)
        dst[:, cols(i, 0)] = t[:span]
        dst[:, cols(i, span)] = t[span:]

    def their_tile(src, dst, i):
        t = dot_t(src[0, rows(i), :], left[:, :depth]) + dot_t(src[1, rows(i), :], left[:, depth:])
        dst[rows(i), :] = t.astype(BF16)

    def their_pair(src, dst, i):
        t = dot_t(src[0, rows(i), :], left[:, :depth]) + dot_t(src[1, rows(i), :], left[:, depth:])
        t = t.astype(BF16)
        dst[0, rows(i), :] = t[:, :span]
        dst[1, rows(i), :] = t[:, span:]

    def put(t, k, i, j):
        return pltpu.make_async_copy(
            res.at[t, k, :, rows(i), :], out.at[t, k, :, rows(i), :], out_sem.at[j * pieces + i]
        )

    def emit(t, k, src, i, j):
        store(t, k, dot_t(src[rows(i), :], weights[...]), i, j)

    def emit_pair(t, k, src, i, j):
        f = dot_t(src[0, rows(i), :], weights[:, :span])
        store(t, k, f + dot_t(src[1, rows(i), :], weights[:, span:]), i, j)

    def store(t, k, f, i, j):
        res[t, k, 0, rows(i), :] = (rec_v[t, k, 0, rows(i), :].astype(F32) - f[:, :span]).astype(BF16)
        res[t, k, 1, rows(i), :] = (rec_v[t, k, 1, rows(i), :].astype(F32) - f[:, span:]).astype(BF16)
        put(t, k, i, j).start()

    def each(body):
        def step(i, carry):
            body(i)
            return carry
        lax.fori_loop(0, pieces, step, 0)

    load.wait()

    @each
    def _(i):
        mate_copy(i).wait_recv()
        own_tile(buf_m, tile, i)

    each(lambda i: emit(0, core, tile, i, 0))

    @pl.when(owner)
    def _():
        @each
        def _(i):
            z_copy(i).wait_recv()
            fwd_copy(i).start()

            @pl.when(i == pieces // 2)
            def _():
                pl.semaphore_signal(go_sem, inc=1, device_id={"shot": mate}, device_id_type=MESH)

            their_tile(buf_a, send_a, i)
            tile_a(i).start()
            row_copy(i).wait_recv()
            share_c(i).start()
            their_pair(buf_c, send_x, i)
            tile_c(i).start()
            own_tile(buf_c, tile3, i)
            own_tile(buf_a, tile, i)

        @each
        def _(i):
            emit(1, side, tile3, i, 3)
            emit(2, side, tile, i, 1)

        fwd_copy(0).wait_recv()
        t = dot_t(left[:, :depth], buf_b[0, :STEP, :]) + dot_t(left[:, depth:], buf_b[1, :STEP, :])
        t = t.astype(BF16)
        recv_x[0, :, :STEP] = t[:span]
        recv_x[1, :, :STEP] = t[span:]

        @each
        def _(i):
            share_b(i).wait_recv()
            own_tile(buf_d, tile2, i)

        each(lambda i: emit(0, 1 - core, tile2, i, 4))

        @each
        def _(i):
            tile_a(i).wait_recv()
            emit(2, 1 - side, recv_a, i, 5)
            tile_b(i).wait_recv()
            emit_pair(1, 1 - side, recv_x, i, 2)

        @each
        def _(i):
            share_c(i).wait_send()
            fwd_copy(i).wait_send()
            tile_c(i).wait_send()

    @pl.when(giver)
    def _():
        pl.semaphore_wait(go_sem, 1)
        for i in range(pieces):
            z_copy(i).start()

        @each
        def _(i):
            fwd_copy(i).wait_recv()
            share_b(i).start()
            their_pair(buf_b, send_x, i)
            tile_b(i).start()
            z_copy(i).wait_recv()

            @pl.when(i == 0)
            def _():
                fwd_copy(0).start()

            their_tile(buf_a, send_a, i)
            tile_a(i).start()
            own_tile(buf_a, tile, i)
            own_tile(buf_b, tile2, i)
            share_c(i).wait_recv()
            own_tile(buf_d, tile3, i)

        @each
        def _(i):
            emit(2, side, tile, i, 1)
            emit(0, 1 - core, tile3, i, 4)
            emit(1, 1 - side, tile2, i, 2)

        @each
        def _(i):
            tile_c(i).wait_recv()
            emit_pair(1, side, recv_x, i, 3)

        @each
        def _(i):
            tile_a(i).wait_recv()
            emit(2, 1 - side, recv_a, i, 5)

        fwd_copy(0).wait_send()

        @each
        def _(i):
            row_copy(i).wait_send()
            share_b(i).wait_send()
            tile_b(i).wait_send()

    @each
    def _(i):
        z_copy(i).wait_send()
        mate_copy(i).wait_send()
        tile_a(i).wait_send()
        put(0, core, i, 0).wait()
        put(2, side, i, 1).wait()
        put(1, 1 - side, i, 2).wait()
        put(1, side, i, 3).wait()
        put(0, 1 - core, i, 4).wait()
        put(2, 1 - side, i, 5).wait()


def ladder(wavefield, recorded, match_filter):
    n = lax.axis_size("shot")
    _, span, depth = wavefield.shape
    pieces = span // STEP
    slots = recorded.shape[0]
    width = -(-(span + match_filter.shape[1]) // STEP) * STEP
    block = pltpu.VMEM((2, span, depth), BF16)
    flat = pltpu.VMEM((span, 2 * span), BF16)
    pair = pltpu.VMEM((2, span, span), BF16)
    return pl.pallas_call(
        functools.partial(kernel, n),
        out_shape=jax.ShapeDtypeStruct(recorded.shape, recorded.dtype),
        in_specs=[
            pl.BlockSpec(memory_space=pltpu.HBM),
            pl.BlockSpec(memory_space=pltpu.HBM),
            pl.BlockSpec(memory_space=pltpu.HBM),
        ],
        out_specs=pl.BlockSpec(memory_space=pl.ANY),
        scratch_shapes=[
            pltpu.VMEM(match_filter.shape, BF16),
            block,
            pltpu.VMEM((2 * span, 2 * depth), BF16),
            pltpu.VMEM((2 * span, 2 * span), BF16),
            block, block, block, block, block,
            flat, pair, flat, pair, flat, flat, flat,
            pltpu.VMEM(recorded.shape, BF16),
            pltpu.VMEM(recorded.shape, BF16),
            pltpu.VMEM((8, width), F32),
            pltpu.SemaphoreType.DMA((7 * pieces,)),
            pltpu.SemaphoreType.DMA((7 * pieces,)),
            pltpu.SemaphoreType.DMA((3,)),
            pltpu.SemaphoreType.DMA((2 * slots * pieces,)),
            pltpu.SemaphoreType.REGULAR,
        ],
        compiler_params=pltpu.CompilerParams(
            collective_id=0, has_side_effects=True, vmem_limit_bytes=LIMIT
        ),
    )(*(pltpu.with_memory_space_constraint(x, pltpu.HBM) for x in (match_filter, wavefield, recorded)))


def passed_along(value, axis, steps):
    count = lax.axis_size(axis)
    pairs = [(source, (source + steps) % count) for source in range(count)]
    return lax.ppermute(value, axis, pairs)


def toeplitz(match_filter, block_span_width):
    tap_count = match_filter.shape[1]
    half_taps = (tap_count - 1) // 2
    row_index = lax.broadcasted_iota(jnp.int32, (block_span_width, block_span_width), 0)
    col_index = lax.broadcasted_iota(jnp.int32, (block_span_width, block_span_width), 1)
    lag_index = row_index - col_index + half_taps
    coeffs = match_filter.astype(jnp.float32)

    def place_tap(tap_index, carried):
        column = lax.dynamic_slice_in_dim(coeffs, tap_index, 1, 1)
        return jnp.where((lag_index == tap_index)[None], column[:, :, None], carried)

    return lax.fori_loop(
        0, tap_count, place_tap, jnp.zeros((2, block_span_width, block_span_width), jnp.float32)
    )


def filter_weights(match_filter, block_span_width):
    toe_pair = toeplitz(match_filter, block_span_width)
    real_component = toe_pair[0].astype(jnp.bfloat16)
    imag_part = toe_pair[1].astype(jnp.bfloat16)
    return jnp.stack(
        [jnp.stack([real_component, imag_part], 1), jnp.stack([-imag_part, real_component], 1)], 0
    )


def shards(wavefield, recorded, match_filter):
    cycle_size = lax.axis_size("shot")
    doubling = cycle_size // 8 == 2 and cycle_size // 4 == 4
    if doubling and cycle_size % 4 == 0 and wavefield.shape[1] % STEP == 0 and wavefield.shape[1] > STEP:
        return ladder(wavefield, recorded, match_filter)
    block_span_width = wavefield.shape[1]
    weights = filter_weights(match_filter, block_span_width)
    real_component = wavefield[0]
    imag_part = wavefield[1]
    left_rows = jnp.concatenate(
        [
            jnp.concatenate([real_component, -imag_part], 1),
            jnp.concatenate([imag_part, real_component], 1),
        ],
        0,
    )
    results = []
    for slot_index, offset in enumerate((1, cycle_size // 8, cycle_size // 4)):
        ahead_data = passed_along(wavefield, "shot", -offset)
        right_rows = jnp.concatenate([ahead_data[0], ahead_data[1]], 1)
        stacked = lax.dot_general(
            left_rows, right_rows, (((1,), (1,)), ((), ())), preferred_element_type=jnp.float32
        )
        forward_tile = stacked.astype(jnp.bfloat16).reshape(2, block_span_width, block_span_width)
        ahead_filtered = jnp.einsum(
            "csq,cqdx->dsx", forward_tile, weights, preferred_element_type=jnp.float32
        )
        received = passed_along(forward_tile, "shot", offset)
        behind_filtered = jnp.einsum(
            "csr,csdx->drx", received, weights, preferred_element_type=jnp.float32
        )
        ahead_out = (recorded[slot_index, 0].astype(jnp.float32) - ahead_filtered).astype(
            jnp.bfloat16
        )
        behind_out = (recorded[slot_index, 1].astype(jnp.float32) - behind_filtered).astype(
            jnp.bfloat16
        )
        results.append(jnp.stack([ahead_out, behind_out]))
    return jnp.stack(results)


def solution(mesh):
    return jax.shard_map(
        shards,
        mesh=mesh,
        in_specs=(P("freq", "shot", None), P("freq", None, None, "shot", None), P()),
        out_specs=P("freq", None, None, "shot", None),
        check_vma=False,
    )
```

```python
import functools

import jax
import jax.numpy as jnp
from jax import lax
from jax.experimental import pallas as pl
from jax.experimental.pallas import tpu as pltpu
from jax.sharding import PartitionSpec as P

MESH = pl.DeviceIdType.MESH
STEP = 128
CH_A, CH_B, CH_C, CH_M, CH_D, CH_TA, CH_TX = range(7)
LIMIT = 40 * 2**20
F32 = jnp.float32
BF16 = jnp.bfloat16


def dot_t(a, b):
    return lax.dot_general(a, b, (((1,), (1,)), ((), ())), preferred_element_type=F32)


def kernel(
    n, mf_hbm, wave, rec, out,
    mf, wave_v, left, weights, buf_a, buf_b, buf_c, buf_m, buf_d,
    send_a, send_x, recv_a, recv_x, tile, tile2, tile3, rec_v, res, taps_row,
    ssem, rsem, in_sem, out_sem,
):
    span, depth = wave_v.shape[1], wave_v.shape[2]
    pieces = span // STEP
    half = (mf.shape[1] - 1) // 2
    me = lax.axis_index("shot")
    core = lax.rem(me, 2)
    side = lax.rem(me // 2, 2)
    mate = me + 1 - 2 * core
    across = me + 2 - 4 * side
    beyond = lax.rem(me + n - 2 + 4 * side, n)
    up, down = lax.rem(me + 4, n), lax.rem(me + n - 4, n)
    z_to = (1 - side) * down + side * up
    z_from = (1 - side) * up + side * down
    owner = (core == side)
    giver = (core != side)

    load_taps = pltpu.make_async_copy(mf_hbm, mf, in_sem.at[2])
    load_taps.start()
    load_wave = pltpu.make_async_copy(wave, wave_v, in_sem.at[0])
    load_wave.start()
    load = pltpu.make_async_copy(rec, rec_v, in_sem.at[1])
    load.start()

    barrier = pltpu.get_barrier_semaphore()
    for other in (mate, across, beyond, up, down):
        pl.semaphore_signal(barrier, inc=1, device_id={"shot": other}, device_id_type=MESH)
    pl.semaphore_wait(barrier, 5)

    def remote(src, dst, sem, target):
        return pltpu.make_async_remote_copy(
            src_ref=src, dst_ref=dst, send_sem=ssem.at[sem], recv_sem=rsem.at[sem],
            device_id={"shot": target}, device_id_type=MESH,
        )

    def rows(i):
        if isinstance(i, int):
            return pl.ds(i * STEP, STEP)
        return pl.ds(pl.multiple_of(i * STEP, STEP), STEP)

    def cols(i, base):
        return pl.ds(pl.multiple_of(base + i * STEP, STEP), STEP)

    def piece(src, dst, channel, i, target):
        return remote(
            src.at[:, rows(i), :], dst.at[:, rows(i), :], channel * pieces + i, target
        )

    def tile_piece(src, dst, channel, i, target):
        return remote(src.at[rows(i), :], dst.at[rows(i), :], channel * pieces + i, target)

    def z_copy(i):
        return piece(wave, buf_a, CH_A, i, z_to)

    def fwd_copy(i):
        return piece(buf_a, buf_b, CH_B, i, across)

    def row_copy(i):
        return piece(wave, buf_c, CH_C, i, across)

    def mate_copy(i):
        return piece(wave, buf_m, CH_M, i, mate)

    def share_c(i):
        return piece(buf_c, buf_d, CH_D, i, mate)

    def share_b(i):
        return piece(buf_b, buf_d, CH_D, i, mate)

    def tile_a(i):
        return tile_piece(send_a, recv_a, CH_TA, i, z_from)

    tail = pl.ds(STEP, span - STEP)

    def tile_b(i):
        return remote(
            send_x.at[:, rows(i), tail], recv_x.at[:, rows(i), tail], CH_TX * pieces + i, beyond
        )

    def tile_c(i):
        return piece(send_x, recv_x, CH_TX, i, across)

    @pl.when(giver)
    def _():
        for i in range(pieces):
            row_copy(i).start()

    for i in range(pieces):
        z_copy(i).start()
    for i in range(pieces):
        mate_copy(i).start()

    load_taps.wait()
    width = taps_row.shape[1]
    taps_row[...] = jnp.zeros_like(taps_row)
    taps_row[0:2, 0:mf.shape[1]] = mf[...].astype(F32)
    row_id = lax.broadcasted_iota(jnp.int32, (span, width), 0)
    banded = []
    for c in range(2):
        x = jnp.broadcast_to(taps_row[c:c + 1, :], (span, width))
        x = pltpu.roll(x, width - half, 1)
        bit = 1
        while bit < span:
            x = jnp.where((row_id // bit) % 2 == 1, pltpu.roll(x, bit, 1), x)
            bit *= 2
        banded.append(x[:, :span].astype(BF16))
    weights[:span, :span] = banded[0]
    weights[:span, span:] = -banded[1]
    weights[span:, :span] = banded[1]
    weights[span:, span:] = banded[0]

    load_wave.wait()
    left[:span, :depth] = wave_v[0]
    left[:span, depth:] = -wave_v[1]
    left[span:, :depth] = wave_v[1]
    left[span:, depth:] = wave_v[0]

    def own_tile(src, dst, i):
        t = dot_t(left[:, :depth], src[0, rows(i), :]) + dot_t(left[:, depth:], src[1, rows(i), :])
        t = t.astype(BF16)
        dst[:, cols(i, 0)] = t[:span]
        dst[:, cols(i, span)] = t[span:]

    def their_tile(src, dst, i):
        t = dot_t(src[0, rows(i), :], left[:, :depth]) + dot_t(src[1, rows(i), :], left[:, depth:])
        dst[rows(i), :] = t.astype(BF16)

    def their_pair(src, dst, i):
        t = dot_t(src[0, rows(i), :], left[:, :depth]) + dot_t(src[1, rows(i), :], left[:, depth:])
        t = t.astype(BF16)
        dst[0, rows(i), :] = t[:, :span]
        dst[1, rows(i), :] = t[:, span:]

    def put(t, k, i, j):
        return pltpu.make_async_copy(
            res.at[t, k, :, rows(i), :], out.at[t, k, :, rows(i), :], out_sem.at[j * pieces + i]
        )

    def emit(t, k, src, i, j):
        store(t, k, dot_t(src[rows(i), :], weights[...]), i, j)

    def emit_pair(t, k, src, i, j):
        f = dot_t(src[0, rows(i), :], weights[:, :span])
        store(t, k, f + dot_t(src[1, rows(i), :], weights[:, span:]), i, j)

    def store(t, k, f, i, j):
        res[t, k, 0, rows(i), :] = (rec_v[t, k, 0, rows(i), :].astype(F32) - f[:, :span]).astype(BF16)
        res[t, k, 1, rows(i), :] = (rec_v[t, k, 1, rows(i), :].astype(F32) - f[:, span:]).astype(BF16)
        put(t, k, i, j).start()

    def each(body):
        def step(i, carry):
            body(i)
            return carry
        lax.fori_loop(0, pieces, step, 0)

    load.wait()

    @each
    def _(i):
        mate_copy(i).wait_recv()
        own_tile(buf_m, tile, i)

    each(lambda i: emit(0, core, tile, i, 0))

    @pl.when(owner)
    def _():
        @each
        def _(i):
            z_copy(i).wait_recv()
            fwd_copy(i).start()

            their_tile(buf_a, send_a, i)
            tile_a(i).start()
            row_copy(i).wait_recv()
            share_c(i).start()
            their_pair(buf_c, send_x, i)
            tile_c(i).start()
            own_tile(buf_c, tile3, i)
            own_tile(buf_a, tile, i)

        @each
        def _(i):
            emit(1, side, tile3, i, 3)
            emit(2, side, tile, i, 1)

        fwd_copy(0).wait_recv()
        t = dot_t(left[:, :depth], buf_b[0, :STEP, :]) + dot_t(left[:, depth:], buf_b[1, :STEP, :])
        t = t.astype(BF16)
        recv_x[0, :, :STEP] = t[:span]
        recv_x[1, :, :STEP] = t[span:]

        @each
        def _(i):
            share_b(i).wait_recv()
            own_tile(buf_d, tile2, i)

        each(lambda i: emit(0, 1 - core, tile2, i, 4))

        @each
        def _(i):
            tile_a(i).wait_recv()
            emit(2, 1 - side, recv_a, i, 5)
            tile_b(i).wait_recv()
            emit_pair(1, 1 - side, recv_x, i, 2)

        @each
        def _(i):
            share_c(i).wait_send()
            fwd_copy(i).wait_send()
            tile_c(i).wait_send()

    @pl.when(giver)
    def _():
        def step(i, carry):
            @pl.when(i < pieces)
            def _():
                z_copy(i).wait_recv()

                @pl.when(i == 0)
                def _():
                    fwd_copy(0).start()

                their_tile(buf_a, send_a, i)
                tile_a(i).start()

            @pl.when(i > 0)
            def _():
                fwd_copy(i - 1).wait_recv()
                share_b(i - 1).start()
                their_pair(buf_b, send_x, i - 1)
                tile_b(i - 1).start()
                own_tile(buf_b, tile2, i - 1)

            @pl.when(i < pieces)
            def _():
                own_tile(buf_a, tile, i)
                share_c(i).wait_recv()
                own_tile(buf_d, tile3, i)

            return carry

        lax.fori_loop(0, pieces + 1, step, 0)

        @each
        def _(i):
            emit(2, side, tile, i, 1)
            emit(0, 1 - core, tile3, i, 4)
            emit(1, 1 - side, tile2, i, 2)

        @each
        def _(i):
            tile_c(i).wait_recv()
            emit_pair(1, side, recv_x, i, 3)

        @each
        def _(i):
            tile_a(i).wait_recv()
            emit(2, 1 - side, recv_a, i, 5)

        fwd_copy(0).wait_send()

        @each
        def _(i):
            row_copy(i).wait_send()
            share_b(i).wait_send()
            tile_b(i).wait_send()

    @each
    def _(i):
        z_copy(i).wait_send()
        mate_copy(i).wait_send()
        tile_a(i).wait_send()
        put(0, core, i, 0).wait()
        put(2, side, i, 1).wait()
        put(1, 1 - side, i, 2).wait()
        put(1, side, i, 3).wait()
        put(0, 1 - core, i, 4).wait()
        put(2, 1 - side, i, 5).wait()


def ladder(wavefield, recorded, match_filter):
    n = lax.axis_size("shot")
    _, span, depth = wavefield.shape
    pieces = span // STEP
    slots = recorded.shape[0]
    width = -(-(span + match_filter.shape[1]) // STEP) * STEP
    block = pltpu.VMEM((2, span, depth), BF16)
    flat = pltpu.VMEM((span, 2 * span), BF16)
    pair = pltpu.VMEM((2, span, span), BF16)
    return pl.pallas_call(
        functools.partial(kernel, n),
        out_shape=jax.ShapeDtypeStruct(recorded.shape, recorded.dtype),
        in_specs=[
            pl.BlockSpec(memory_space=pltpu.HBM),
            pl.BlockSpec(memory_space=pltpu.HBM),
            pl.BlockSpec(memory_space=pltpu.HBM),
        ],
        out_specs=pl.BlockSpec(memory_space=pl.ANY),
        scratch_shapes=[
            pltpu.VMEM(match_filter.shape, BF16),
            block,
            pltpu.VMEM((2 * span, 2 * depth), BF16),
            pltpu.VMEM((2 * span, 2 * span), BF16),
            block, block, block, block, block,
            flat, pair, flat, pair, flat, flat, flat,
            pltpu.VMEM(recorded.shape, BF16),
            pltpu.VMEM(recorded.shape, BF16),
            pltpu.VMEM((8, width), F32),
            pltpu.SemaphoreType.DMA((7 * pieces,)),
            pltpu.SemaphoreType.DMA((7 * pieces,)),
            pltpu.SemaphoreType.DMA((3,)),
            pltpu.SemaphoreType.DMA((2 * slots * pieces,)),
        ],
        compiler_params=pltpu.CompilerParams(
            collective_id=0, has_side_effects=True, vmem_limit_bytes=LIMIT
        ),
    )(*(pltpu.with_memory_space_constraint(x, pltpu.HBM) for x in (match_filter, wavefield, recorded)))


def passed_along(value, axis, steps):
    count = lax.axis_size(axis)
    pairs = [(source, (source + steps) % count) for source in range(count)]
    return lax.ppermute(value, axis, pairs)


def toeplitz(match_filter, block_span_width):
    tap_count = match_filter.shape[1]
    half_taps = (tap_count - 1) // 2
    row_index = lax.broadcasted_iota(jnp.int32, (block_span_width, block_span_width), 0)
    col_index = lax.broadcasted_iota(jnp.int32, (block_span_width, block_span_width), 1)
    lag_index = row_index - col_index + half_taps
    coeffs = match_filter.astype(jnp.float32)

    def place_tap(tap_index, carried):
        column = lax.dynamic_slice_in_dim(coeffs, tap_index, 1, 1)
        return jnp.where((lag_index == tap_index)[None], column[:, :, None], carried)

    return lax.fori_loop(
        0, tap_count, place_tap, jnp.zeros((2, block_span_width, block_span_width), jnp.float32)
    )


def filter_weights(match_filter, block_span_width):
    toe_pair = toeplitz(match_filter, block_span_width)
    real_component = toe_pair[0].astype(jnp.bfloat16)
    imag_part = toe_pair[1].astype(jnp.bfloat16)
    return jnp.stack(
        [jnp.stack([real_component, imag_part], 1), jnp.stack([-imag_part, real_component], 1)], 0
    )


def shards(wavefield, recorded, match_filter):
    cycle_size = lax.axis_size("shot")
    doubling = cycle_size // 8 == 2 and cycle_size // 4 == 4
    if doubling and cycle_size % 4 == 0 and wavefield.shape[1] % STEP == 0 and wavefield.shape[1] > STEP:
        return ladder(wavefield, recorded, match_filter)
    block_span_width = wavefield.shape[1]
    weights = filter_weights(match_filter, block_span_width)
    real_component = wavefield[0]
    imag_part = wavefield[1]
    left_rows = jnp.concatenate(
        [
            jnp.concatenate([real_component, -imag_part], 1),
            jnp.concatenate([imag_part, real_component], 1),
        ],
        0,
    )
    results = []
    for slot_index, offset in enumerate((1, cycle_size // 8, cycle_size // 4)):
        ahead_data = passed_along(wavefield, "shot", -offset)
        right_rows = jnp.concatenate([ahead_data[0], ahead_data[1]], 1)
        stacked = lax.dot_general(
            left_rows, right_rows, (((1,), (1,)), ((), ())), preferred_element_type=jnp.float32
        )
        forward_tile = stacked.astype(jnp.bfloat16).reshape(2, block_span_width, block_span_width)
        ahead_filtered = jnp.einsum(
            "csq,cqdx->dsx", forward_tile, weights, preferred_element_type=jnp.float32
        )
        received = passed_along(forward_tile, "shot", offset)
        behind_filtered = jnp.einsum(
            "csr,csdx->drx", received, weights, preferred_element_type=jnp.float32
        )
        ahead_out = (recorded[slot_index, 0].astype(jnp.float32) - ahead_filtered).astype(
            jnp.bfloat16
        )
        behind_out = (recorded[slot_index, 1].astype(jnp.float32) - behind_filtered).astype(
            jnp.bfloat16
        )
        results.append(jnp.stack([ahead_out, behind_out]))
    return jnp.stack(results)


def solution(mesh):
    return jax.shard_map(
        shards,
        mesh=mesh,
        in_specs=(P("freq", "shot", None), P("freq", None, None, "shot", None), P()),
        out_specs=P("freq", None, None, "shot", None),
        check_vma=False,
    )
```

```python
import functools

import jax
import jax.numpy as jnp
from jax import lax
from jax.experimental import pallas as pl
from jax.experimental.pallas import tpu as pltpu
from jax.sharding import PartitionSpec as P

MESH = pl.DeviceIdType.MESH
STEP = 128
CH_A, CH_B, CH_C, CH_M, CH_D, CH_TA, CH_TX = range(7)
LIMIT = 40 * 2**20
F32 = jnp.float32
BF16 = jnp.bfloat16


def dot_t(a, b):
    return lax.dot_general(a, b, (((1,), (1,)), ((), ())), preferred_element_type=F32)


def kernel(
    n, mf_hbm, wave, rec, out,
    mf, wave_v, left, weights, buf_a, buf_b, buf_c, buf_m, buf_d,
    send_a, send_x, recv_a, recv_x, tile, tile2, tile3, rec_v, res, taps_row,
    ssem, rsem, in_sem, out_sem,
):
    span, depth = wave_v.shape[1], wave_v.shape[2]
    pieces = span // STEP
    half = (mf.shape[1] - 1) // 2
    me = lax.axis_index("shot")
    core = lax.rem(me, 2)
    side = lax.rem(me // 2, 2)
    mate = me + 1 - 2 * core
    across = me + 2 - 4 * side
    beyond = lax.rem(me + n - 2 + 4 * side, n)
    up, down = lax.rem(me + 4, n), lax.rem(me + n - 4, n)
    z_to = (1 - side) * down + side * up
    z_from = (1 - side) * up + side * down
    owner = (core == side)
    giver = (core != side)

    load_taps = pltpu.make_async_copy(mf_hbm, mf, in_sem.at[2])
    load_taps.start()
    load_wave = pltpu.make_async_copy(wave, wave_v, in_sem.at[0])
    load_wave.start()
    load = pltpu.make_async_copy(rec, rec_v, in_sem.at[1])
    load.start()

    barrier = pltpu.get_barrier_semaphore()
    for other in (mate, across, beyond, up, down):
        pl.semaphore_signal(barrier, inc=1, device_id={"shot": other}, device_id_type=MESH)
    pl.semaphore_wait(barrier, 5)

    def remote(src, dst, sem, target):
        return pltpu.make_async_remote_copy(
            src_ref=src, dst_ref=dst, send_sem=ssem.at[sem], recv_sem=rsem.at[sem],
            device_id={"shot": target}, device_id_type=MESH,
        )

    def rows(i):
        if isinstance(i, int):
            return pl.ds(i * STEP, STEP)
        return pl.ds(pl.multiple_of(i * STEP, STEP), STEP)

    def cols(i, base):
        return pl.ds(pl.multiple_of(base + i * STEP, STEP), STEP)

    def piece(src, dst, channel, i, target):
        return remote(
            src.at[:, rows(i), :], dst.at[:, rows(i), :], channel * pieces + i, target
        )

    def tile_piece(src, dst, channel, i, target):
        return remote(src.at[rows(i), :], dst.at[rows(i), :], channel * pieces + i, target)

    def z_copy(i):
        return piece(wave, buf_a, CH_A, i, z_to)

    def fwd_copy(i):
        return piece(buf_a, buf_b, CH_B, i, across)

    def row_copy(i):
        return piece(wave, buf_c, CH_C, i, across)

    def mate_copy(i):
        return piece(wave, buf_m, CH_M, i, mate)

    def share_c(i):
        return piece(buf_c, buf_d, CH_D, i, mate)

    def share_b(i):
        return piece(buf_b, buf_d, CH_D, i, mate)

    def tile_a(i):
        return tile_piece(send_a, recv_a, CH_TA, i, z_from)

    def tile_b(i):
        return tile_piece(send_x, recv_x, CH_TX, i, beyond)

    def tile_c(i):
        return tile_piece(send_x, recv_x, CH_TX, i, across)

    @pl.when(giver)
    def _():
        for i in range(pieces):
            row_copy(i).start()

    for i in range(pieces):
        z_copy(i).start()
    for i in range(pieces):
        mate_copy(i).start()

    load_taps.wait()
    width = taps_row.shape[1]
    taps_row[...] = jnp.zeros_like(taps_row)
    taps_row[0:2, 0:mf.shape[1]] = mf[...].astype(F32)
    row_id = lax.broadcasted_iota(jnp.int32, (span, width), 0)
    banded = []
    for c in range(2):
        x = jnp.broadcast_to(taps_row[c:c + 1, :], (span, width))
        x = pltpu.roll(x, width - half, 1)
        bit = 1
        while bit < span:
            x = jnp.where((row_id // bit) % 2 == 1, pltpu.roll(x, bit, 1), x)
            bit *= 2
        banded.append(x[:, :span].astype(BF16))
    weights[:span, :span] = banded[0]
    weights[:span, span:] = -banded[1]
    weights[span:, :span] = banded[1]
    weights[span:, span:] = banded[0]

    load_wave.wait()
    left[:span, :depth] = wave_v[0]
    left[:span, depth:] = -wave_v[1]
    left[span:, :depth] = wave_v[1]
    left[span:, depth:] = wave_v[0]

    def own_tile(src, dst, i):
        t = dot_t(left[:, :depth], src[0, rows(i), :]) + dot_t(left[:, depth:], src[1, rows(i), :])
        t = t.astype(BF16)
        dst[:, cols(i, 0)] = t[:span]
        dst[:, cols(i, span)] = t[span:]

    def their_tile(src, dst, i):
        t = dot_t(src[0, rows(i), :], left[:, :depth]) + dot_t(src[1, rows(i), :], left[:, depth:])
        dst[rows(i), :] = t.astype(BF16)

    def put(t, k, i, j):
        return pltpu.make_async_copy(
            res.at[t, k, :, rows(i), :], out.at[t, k, :, rows(i), :], out_sem.at[j * pieces + i]
        )

    def emit(t, k, src, i, j):
        f = dot_t(src[rows(i), :], weights[...])
        res[t, k, 0, rows(i), :] = (rec_v[t, k, 0, rows(i), :].astype(F32) - f[:, :span]).astype(BF16)
        res[t, k, 1, rows(i), :] = (rec_v[t, k, 1, rows(i), :].astype(F32) - f[:, span:]).astype(BF16)
        put(t, k, i, j).start()

    def each(body):
        def step(i, carry):
            body(i)
            return carry
        lax.fori_loop(0, pieces, step, 0)

    load.wait()

    @each
    def _(i):
        mate_copy(i).wait_recv()
        own_tile(buf_m, tile, i)

    each(lambda i: emit(0, core, tile, i, 0))

    @pl.when(owner)
    def _():
        @each
        def _(i):
            row_copy(i).wait_recv()
            share_c(i).start()
            z_copy(i).wait_recv()
            fwd_copy(i).start()
            their_tile(buf_c, send_x, i)
            tile_c(i).start()
            their_tile(buf_a, send_a, i)

            @pl.when(i == pieces - 1)
            def _():
                for j in range(pieces):
                    tile_a(j).start()

            own_tile(buf_c, tile3, i)
            own_tile(buf_a, tile, i)

        @each
        def _(i):
            emit(1, side, tile3, i, 3)
            emit(2, side, tile, i, 1)

        @each
        def _(i):
            share_b(i).wait_recv()
            own_tile(buf_d, tile2, i)

        each(lambda i: emit(0, 1 - core, tile2, i, 4))

        @each
        def _(i):
            tile_a(i).wait_recv()
            emit(2, 1 - side, recv_a, i, 5)
            tile_b(i).wait_recv()
            emit(1, 1 - side, recv_x, i, 2)

        @each
        def _(i):
            share_c(i).wait_send()
            fwd_copy(i).wait_send()
            tile_c(i).wait_send()

    @pl.when(giver)
    def _():
        @each
        def _(i):
            z_copy(i).wait_recv()
            their_tile(buf_a, send_a, i)

            @pl.when(i == pieces - 1)
            def _():
                for j in range(pieces):
                    tile_a(j).start()

            own_tile(buf_a, tile, i)
            share_c(i).wait_recv()
            own_tile(buf_d, tile3, i)
            fwd_copy(i).wait_recv()
            share_b(i).start()
            their_tile(buf_b, send_x, i)
            tile_b(i).start()
            own_tile(buf_b, tile2, i)

        @each
        def _(i):
            emit(2, side, tile, i, 1)
            emit(0, 1 - core, tile3, i, 4)
            emit(1, 1 - side, tile2, i, 2)

        @each
        def _(i):
            tile_c(i).wait_recv()
            emit(1, side, recv_x, i, 3)

        @each
        def _(i):
            tile_a(i).wait_recv()
            emit(2, 1 - side, recv_a, i, 5)

        @each
        def _(i):
            row_copy(i).wait_send()
            share_b(i).wait_send()
            tile_b(i).wait_send()

    @each
    def _(i):
        z_copy(i).wait_send()
        mate_copy(i).wait_send()
        tile_a(i).wait_send()
        put(0, core, i, 0).wait()
        put(2, side, i, 1).wait()
        put(1, 1 - side, i, 2).wait()
        put(1, side, i, 3).wait()
        put(0, 1 - core, i, 4).wait()
        put(2, 1 - side, i, 5).wait()


def ladder(wavefield, recorded, match_filter):
    n = lax.axis_size("shot")
    _, span, depth = wavefield.shape
    pieces = span // STEP
    slots = recorded.shape[0]
    width = -(-(span + match_filter.shape[1]) // STEP) * STEP
    block = pltpu.VMEM((2, span, depth), BF16)
    flat = pltpu.VMEM((span, 2 * span), BF16)
    return pl.pallas_call(
        functools.partial(kernel, n),
        out_shape=jax.ShapeDtypeStruct(recorded.shape, recorded.dtype),
        in_specs=[
            pl.BlockSpec(memory_space=pltpu.HBM),
            pl.BlockSpec(memory_space=pltpu.HBM),
            pl.BlockSpec(memory_space=pltpu.HBM),
        ],
        out_specs=pl.BlockSpec(memory_space=pl.ANY),
        scratch_shapes=[
            pltpu.VMEM(match_filter.shape, BF16),
            block,
            pltpu.VMEM((2 * span, 2 * depth), BF16),
            pltpu.VMEM((2 * span, 2 * span), BF16),
            block, block, block, block, block,
            flat, flat, flat, flat, flat, flat, flat,
            pltpu.VMEM(recorded.shape, BF16),
            pltpu.VMEM(recorded.shape, BF16),
            pltpu.VMEM((8, width), F32),
            pltpu.SemaphoreType.DMA((7 * pieces,)),
            pltpu.SemaphoreType.DMA((7 * pieces,)),
            pltpu.SemaphoreType.DMA((3,)),
            pltpu.SemaphoreType.DMA((2 * slots * pieces,)),
        ],
        compiler_params=pltpu.CompilerParams(
            collective_id=0, has_side_effects=True, vmem_limit_bytes=LIMIT
        ),
    )(*(pltpu.with_memory_space_constraint(x, pltpu.HBM) for x in (match_filter, wavefield, recorded)))


def passed_along(value, axis, steps):
    count = lax.axis_size(axis)
    pairs = [(source, (source + steps) % count) for source in range(count)]
    return lax.ppermute(value, axis, pairs)


def toeplitz(match_filter, block_span_width):
    tap_count = match_filter.shape[1]
    half_taps = (tap_count - 1) // 2
    row_index = lax.broadcasted_iota(jnp.int32, (block_span_width, block_span_width), 0)
    col_index = lax.broadcasted_iota(jnp.int32, (block_span_width, block_span_width), 1)
    lag_index = row_index - col_index + half_taps
    coeffs = match_filter.astype(jnp.float32)

    def place_tap(tap_index, carried):
        column = lax.dynamic_slice_in_dim(coeffs, tap_index, 1, 1)
        return jnp.where((lag_index == tap_index)[None], column[:, :, None], carried)

    return lax.fori_loop(
        0, tap_count, place_tap, jnp.zeros((2, block_span_width, block_span_width), jnp.float32)
    )


def filter_weights(match_filter, block_span_width):
    toe_pair = toeplitz(match_filter, block_span_width)
    real_component = toe_pair[0].astype(jnp.bfloat16)
    imag_part = toe_pair[1].astype(jnp.bfloat16)
    return jnp.stack(
        [jnp.stack([real_component, imag_part], 1), jnp.stack([-imag_part, real_component], 1)], 0
    )


def shards(wavefield, recorded, match_filter):
    cycle_size = lax.axis_size("shot")
    doubling = cycle_size // 8 == 2 and cycle_size // 4 == 4
    if doubling and cycle_size % 4 == 0 and wavefield.shape[1] % STEP == 0:
        return ladder(wavefield, recorded, match_filter)
    block_span_width = wavefield.shape[1]
    weights = filter_weights(match_filter, block_span_width)
    real_component = wavefield[0]
    imag_part = wavefield[1]
    left_rows = jnp.concatenate(
        [
            jnp.concatenate([real_component, -imag_part], 1),
            jnp.concatenate([imag_part, real_component], 1),
        ],
        0,
    )
    results = []
    for slot_index, offset in enumerate((1, cycle_size // 8, cycle_size // 4)):
        ahead_data = passed_along(wavefield, "shot", -offset)
        right_rows = jnp.concatenate([ahead_data[0], ahead_data[1]], 1)
        stacked = lax.dot_general(
            left_rows, right_rows, (((1,), (1,)), ((), ())), preferred_element_type=jnp.float32
        )
        forward_tile = stacked.astype(jnp.bfloat16).reshape(2, block_span_width, block_span_width)
        ahead_filtered = jnp.einsum(
            "csq,cqdx->dsx", forward_tile, weights, preferred_element_type=jnp.float32
        )
        received = passed_along(forward_tile, "shot", offset)
        behind_filtered = jnp.einsum(
            "csr,csdx->drx", received, weights, preferred_element_type=jnp.float32
        )
        ahead_out = (recorded[slot_index, 0].astype(jnp.float32) - ahead_filtered).astype(
            jnp.bfloat16
        )
        behind_out = (recorded[slot_index, 1].astype(jnp.float32) - behind_filtered).astype(
            jnp.bfloat16
        )
        results.append(jnp.stack([ahead_out, behind_out]))
    return jnp.stack(results)


def solution(mesh):
    return jax.shard_map(
        shards,
        mesh=mesh,
        in_specs=(P("freq", "shot", None), P("freq", None, None, "shot", None), P()),
        out_specs=P("freq", None, None, "shot", None),
        check_vma=False,
    )
```
